32 devices in a mesh: grp: 4 (over z), ex: 8 (over y, x, core).
Axes of the slice: x: 2, y: 2, z: 4, core: 2. Of those that a mesh axis runs over, the one named last changes fastest.
Arguments:
- tokens: bfloat16 [2048, 3584], P(('grp', 'ex')), may hold values from -6 to 6
- expert_ids: int32 [2048, 8], P(('grp', 'ex')), may hold values from 0 to 15, all different within a row; in each aligned block of 64 rows (0 to 63, 64 to 127, ...) at most 40 rows name the same one
- combine: float32 [2048, 8], P(('grp', 'ex')), may hold values from 0.25 to 0.5
- hot_flags: int32 [16], replicated, may hold values from 0 to 1
- gate_up_weight: bfloat16 [4, 8, 2, 3584, 512], P('grp', 'ex'), as said below
- gate_up_scale: float32 [4, 8, 2, 28, 512], P('grp', 'ex')
- down_weight: bfloat16 [4, 8, 512, 3584], P('grp', 'ex'), as said below
- down_scale: float32 [4, 8, 4, 3584], P('grp', 'ex')
Outputs:
- moe_out: bfloat16 [2048, 3584], P(('grp', 'ex'))
The draws below stay inside these ranges and needn't reach their ends.
Inputs may be any that keep to these rules, and one draw needn't show every extreme that they name: `expert_ids`: each row names 8 different experts; the 64 rows of one device name one expert at most 40 times. `gate_up_weight`: for an expert whose hot flag is 0, every entry is an integer from -8 to 7. `down_weight`: for an expert whose hot flag is 0, every entry is an integer from -8 to 7.
All inputs are finite; a program needn't handle non-finite values.
Results may differ from the reference program's by a relative error of at most 0.008.
Values may be sent and summed in bfloat16 or wider, within the bound.
A program may use at most 128 MiB of HBM per device.

```python
import math
import jax
import jax.numpy as jnp
import numpy as np
from jax import lax

D = 3584
FF = 1024
TOP = 8
GROUP = 128
TOK_DEV = 64
SLABS = 4
LANES = 8
EXPERTS = 16
FFH = 512
CAP = 40
TOKENS = 2048
N_GRP = 4
N_EX = 8


def flag_table(key):
    levels = jax.random.randint(jax.random.fold_in(key, 11), (EXPERTS,), 0, 2)
    return levels.astype(jnp.int32)


def slab_flags(key):
    flags = flag_table(key)
    pair_index = jnp.arange(SLABS, dtype=jnp.int32) // 2
    lane_index = jnp.arange(LANES, dtype=jnp.int32)
    return flags[pair_index[:, None] * LANES + lane_index[None, :]]


def mixed_weights(key, shape, fan_in, extra_dims):
    is_hot = slab_flags(key).reshape((SLABS, LANES) + (1,) * extra_dims) == 1
    real_key = jax.random.fold_in(key, 21)
    dense = jax.random.normal(real_key, shape, jnp.float32) * fan_in ** (-0.5)
    codes = jax.random.randint(jax.random.fold_in(key, 22), shape, -8, 8).astype(jnp.float32)
    return jnp.where(is_hot, dense, codes).astype(jnp.bfloat16)


def spread_scales(key, shape, fan_in):
    low_end, high_end = (math.log(0.5), math.log(2.0))
    logs = jax.random.uniform(jax.random.fold_in(key, 31), shape, jnp.float32, low_end, high_end)
    return (jnp.exp(logs) * (0.22 * fan_in ** (-0.5))).astype(jnp.float32)


def draw_hot_flags(key, part):
    return flag_table(key)


def draw_gate_up_weight(key, part):
    return mixed_weights(key, (SLABS, LANES, 2, D, FFH), D, 3)


def draw_down_weight(key, part):
    return mixed_weights(key, (SLABS, LANES, FFH, D), FF, 2)


def draw_gate_up_scale(key, part):
    return spread_scales(key, (SLABS, LANES, 2, D // GROUP, FFH), D)


def draw_down_scale(key, part):
    return spread_scales(key, (SLABS, LANES, FFH // GROUP, D), FF)


def level_of(rng, dims, cuts, low, top_value):
    factor_of = 1.0
    for position, parts in cuts:
        draws = jax.random.uniform(jax.random.fold_in(jax.random.fold_in(rng, 6), position), (parts,), jnp.float32, low / len(cuts), top_value / len(cuts))
        factor_of = factor_of * jnp.repeat(jnp.exp(draws), dims[position] // parts).reshape((-1,) + (1,) * (len(dims) - 1 - position))
    return factor_of


def routed_block(own_key, own, number, rows, number_of, top, reach, skew):
    ranking = jax.random.permutation(own_key, number_of)
    heavy_load, common = shares(number_of, rows * top, reach, skew, True), shares(number_of, rows * top, reach, skew, False)
    places = jnp.arange(number_of)

    def named(sizes, rotation):
        used = int((sizes > 0).sum())
        fixed = max(1, used // 4)
        passed = fixed + (places - fixed + rotation * (used - fixed)) % max(1, number_of - fixed)
        return jnp.zeros((number_of,), jnp.int32).at[ranking[jnp.where(places < fixed, places, passed)]].set(jnp.asarray(sizes, jnp.int32))

    sizes = jnp.where(number % 4 == 0, named(heavy_load, number // 4), named(common, number - number // 4 - 1))
    mixed = jax.random.permutation(jax.random.fold_in(own, 3), number_of)
    source_of, sink = mixed[0:number_of // 2 * 2:2], mixed[1:number_of // 2 * 2:2]
    margin = jnp.minimum(sizes[source_of] - 1, reach - sizes[sink]) // 2
    margin = jnp.where((source_of == ranking[0]) | (sink == ranking[0]) | (sizes[sink] == 0), 0, jnp.maximum(margin, 0))
    passed = jax.random.randint(jax.random.fold_in(own, 4), (number_of // 2,), 0, 1 << 20) % (margin + 1)
    sizes = sizes.at[source_of].add(-passed).at[sink].add(passed)
    labels = jnp.searchsorted(jnp.cumsum(sizes), jnp.arange(rows * top), side="right").astype(jnp.int32)
    grid = labels.reshape(top, rows).T
    grid = grid[jax.random.permutation(jax.random.fold_in(own, 1), rows)]
    rotation = jax.random.randint(jax.random.fold_in(own, 2), (rows, 1), 0, top)
    return jnp.take_along_axis(grid, (jnp.arange(top)[None, :] + rotation) % top, axis=1)


def shares(number_of, total, bound, slope, full):
    weights = [(1 << 20) // math.isqrt(rank ** slope) + 1 for rank in range(1, number_of + 1)]
    largest = bound if full else min(bound, max(-(-total // number_of), total * weights[0] // sum(weights)))
    least = 1 if total - largest >= number_of - 1 else 0
    holding, rest = [largest] + [least] * (number_of - 1), total - largest - least * (number_of - 1)
    while rest > 0:
        movable = [i for i in range(1, number_of) if holding[i] < largest] or [i for i in range(1, number_of) if holding[i] < bound]
        pool, remaining = sum([weights[i] for i in movable]), rest
        for i in movable:
            more = min(bound - holding[i], max(1, remaining * weights[i] // pool), rest)
            holding[i] = holding[i] + more
            rest = rest - more
    return np.array(holding)


def normal_values(stream_key, dims, scale, reach, shards=(), kind=jnp.bfloat16):
    factor_of = level_of(stream_key, dims, shards, -0.22, 0.18) if shards else 1.0
    array = jax.random.normal(stream_key, dims, jnp.float32) * scale * factor_of
    return jnp.minimum(jnp.maximum(array, -reach), reach).astype(kind)


def setup_inputs(seed: int = 0) -> dict:
    key_list = jax.random.split(jax.random.key(seed), 9)
    tokens = normal_values(key_list[0], (TOKENS, D), 1.0, 6.0, ((0, 32),))
    expert_ids_keys = jax.random.split(jax.random.fold_in(key_list[1], 1), TOKENS // TOK_DEV)
    expert_ids_turns = jax.random.permutation(jax.random.fold_in(key_list[1], 3), TOKENS // TOK_DEV)
    expert_ids = jax.vmap(lambda own, number: routed_block(jax.random.fold_in(key_list[1], 2), own, number, TOK_DEV, EXPERTS, TOP, CAP, 2))(expert_ids_keys, expert_ids_turns).reshape((TOKENS, TOP))
    combine = jnp.clip(0.25 + 0.25 * jax.random.uniform(key_list[2], (TOKENS, TOP), jnp.float32) ** level_of(key_list[2], (TOKENS, TOP), ((0, 32),), -0.2, 0.2), 0.25, 0.5)
    hot_flags = draw_hot_flags(jax.random.fold_in(key_list[8], 71), 0)
    gate_up_weight = draw_gate_up_weight(jax.random.fold_in(key_list[8], 71), 0)
    gate_up_scale = draw_gate_up_scale(jax.random.fold_in(key_list[8], 71), 0)
    down_weight = draw_down_weight(jax.random.fold_in(key_list[8], 71), 0)
    down_scale = draw_down_scale(jax.random.fold_in(key_list[8], 71), 0)
    return {"tokens": tokens, "expert_ids": expert_ids, "combine": combine, "hot_flags": hot_flags, "gate_up_weight": gate_up_weight, "gate_up_scale": gate_up_scale, "down_weight": down_weight, "down_scale": down_scale}


def scale_groups(weights, scales):
    row_count = weights.shape[0]
    group_count = scales.shape[0]
    shaped = weights.reshape(group_count, row_count // group_count, weights.shape[1])
    return (shaped * scales[:, None, :]).reshape(weights.shape)


def dequantize(weights, scales, is_hot):
    scaled = scale_groups(weights, scales).astype(jnp.bfloat16)
    return jnp.where(is_hot, weights, scaled)


def half_expert(token_rows, gate_up, gate_up_scales, down, down_scales, is_hot):
    gate_matrix = dequantize(gate_up[0], gate_up_scales[0], is_hot)
    up_matrix = dequantize(gate_up[1], gate_up_scales[1], is_hot)
    down_matrix = dequantize(down, down_scales, is_hot)
    gate_proj = jnp.dot(token_rows, gate_matrix, preferred_element_type=jnp.float32)
    up_proj = jnp.dot(token_rows, up_matrix, preferred_element_type=jnp.float32)
    hidden = (jax.nn.silu(gate_proj) * up_proj).astype(jnp.bfloat16)
    return jnp.dot(hidden, down_matrix, preferred_element_type=jnp.float32).astype(jnp.bfloat16)


def reference(tokens, expert_ids, combine, hot_flags, gate_up_weight, gate_up_scale, down_weight, down_scale):
    lane_count = N_EX
    expert_count = N_GRP * N_EX // 2
    most_rows = N_GRP * N_EX * CAP
    route_total = TOKENS * TOP
    flat_expert = expert_ids.reshape(route_total)
    flat_token = (jnp.arange(route_total, dtype=jnp.int32) // TOP).astype(jnp.int32)
    flat_weight = combine.reshape(route_total)
    padded_tokens = jnp.concatenate([tokens, jnp.zeros((1, D), tokens.dtype)], axis=0)

    def one_expert(running, expert_id):
        picked = jnp.nonzero(flat_expert == expert_id, size=most_rows, fill_value=route_total)[0].astype(jnp.int32)
        is_valid = picked < route_total
        safe_index = jnp.minimum(picked, route_total - 1).astype(jnp.int32)
        token_index = jnp.where(is_valid, flat_token[safe_index], TOKENS).astype(jnp.int32)
        weights_now = jnp.where(is_valid, flat_weight[safe_index], jnp.zeros((), flat_weight.dtype))
        token_rows = padded_tokens[token_index]
        pair_index = expert_id // lane_count
        lane_index = expert_id % lane_count
        is_hot = hot_flags[expert_id] == 1
        half_sum = jnp.zeros((most_rows, D), jnp.float32)
        for half_index in range(2):
            slab_index = 2 * pair_index + half_index
            partial_value = half_expert(token_rows, gate_up_weight[slab_index, lane_index], gate_up_scale[slab_index, lane_index], down_weight[slab_index, lane_index], down_scale[slab_index, lane_index], is_hot)
            half_sum = half_sum + partial_value.astype(jnp.float32)
        rounded = lax.optimization_barrier(half_sum.astype(jnp.bfloat16)).astype(jnp.float32)
        return running.at[token_index].add(weights_now[:, None] * rounded, mode="drop"), None

    running, unused = lax.scan(one_expert, jnp.zeros((TOKENS, D), jnp.float32), jnp.arange(expert_count, dtype=jnp.int32))
    return running.astype(jnp.bfloat16)
```

```python
import jax
import jax.numpy as jnp
from jax import lax
from jax.sharding import PartitionSpec as P


def dequantize(weights, scales, is_hot):
    group_count = scales.shape[0]
    shaped = weights.reshape(group_count, weights.shape[0] // group_count, weights.shape[1])
    scaled = (shaped * scales[:, None, :]).reshape(weights.shape).astype(jnp.bfloat16)
    return jnp.where(is_hot, weights, scaled)


def routed_shards(
    tokens, expert_ids, combine, hot_flags, gate_up_weight, gate_up_scale, down_weight, down_scale
):
    group_count = lax.axis_size("grp")
    lane_count = lax.axis_size("ex")
    pair_count = group_count // 2
    token_count = tokens.shape[0]
    model_width = tokens.shape[1]
    top_count = expert_ids.shape[1]
    expert_count = pair_count * lane_count
    route_count = token_count * top_count
    capacity = max(2, (5 * route_count + 4 * expert_count - 1) // (4 * expert_count))
    slot_count = expert_count * capacity
    flat_expert = expert_ids.reshape(route_count)
    route_order = jnp.arange(route_count, dtype=jnp.int32)
    earlier = (flat_expert[None, :] == flat_expert[:, None]) & (
        route_order[None, :] < route_order[:, None]
    )
    route_rank = jnp.sum(earlier, axis=1, dtype=jnp.int32)
    slot_of = flat_expert * capacity + route_rank
    slot_match = slot_of[None, :] == jnp.arange(slot_count, dtype=jnp.int32)[:, None]
    filled = jnp.any(slot_match, axis=1)
    source = jnp.sum(jnp.where(slot_match, route_order[None, :] // top_count, 0), axis=1)
    slot_rows = jnp.where(filled[:, None], tokens[source], jnp.zeros((), tokens.dtype))
    outgoing = slot_rows.reshape(pair_count, lane_count, capacity, model_width)
    own_expert = lax.axis_index("grp") // 2 * lane_count + lax.axis_index("ex")
    is_hot = hot_flags[own_expert] == 1
    gate_matrix = dequantize(gate_up_weight[0, 0, 0], gate_up_scale[0, 0, 0], is_hot)
    up_matrix = dequantize(gate_up_weight[0, 0, 1], gate_up_scale[0, 0, 1], is_hot)
    down_matrix = dequantize(down_weight[0, 0], down_scale[0, 0], is_hot)
    pair_index = flat_expert // lane_count
    lane_index = flat_expert % lane_count
    within = lax.all_to_all(outgoing, "ex", split_axis=1, concat_axis=1, tiled=True)
    doubled = jnp.repeat(within, 2, axis=0)
    arrived_block = lax.all_to_all(doubled, "grp", split_axis=0, concat_axis=0, tiled=True)
    flat_rows = arrived_block.reshape(-1, model_width)
    gate_proj = jnp.dot(flat_rows, gate_matrix, preferred_element_type=jnp.float32)
    up_proj = jnp.dot(flat_rows, up_matrix, preferred_element_type=jnp.float32)
    hidden = (jax.nn.silu(gate_proj) * up_proj).astype(jnp.bfloat16)
    partial_value = jnp.dot(hidden, down_matrix, preferred_element_type=jnp.float32).astype(
        jnp.bfloat16
    )
    across = lax.all_to_all(
        partial_value.reshape(arrived_block.shape), "grp", split_axis=0, concat_axis=0, tiled=True
    )
    returned = lax.all_to_all(across, "ex", split_axis=1, concat_axis=1, tiled=True)
    flat_back = returned.reshape(-1, model_width)
    first_index = (2 * pair_index * lane_count + lane_index) * capacity + route_rank
    second_index = first_index + lane_count * capacity
    both_halves = flat_back[first_index].astype(jnp.float32) + flat_back[second_index].astype(
        jnp.float32
    )
    expert_rows = lax.optimization_barrier(both_halves.astype(jnp.bfloat16)).astype(jnp.float32)
    weighted = expert_rows * combine.reshape(route_count)[:, None]
    return jnp.sum(weighted.reshape(token_count, top_count, model_width), axis=1).astype(
        jnp.bfloat16
    )


def dense_shards(
    tokens, expert_ids, combine, hot_flags, gate_up_weight, gate_up_scale, down_weight, down_scale
):
    lane_count = lax.axis_size("ex")
    expert_count = lax.axis_size("grp") // 2 * lane_count
    own_expert = lax.axis_index("grp") // 2 * lane_count + lax.axis_index("ex")
    is_hot = hot_flags[own_expert] == 1
    named = expert_ids[:, :, None] == jnp.arange(expert_count, dtype=jnp.int32)
    coefficient = jnp.sum(jnp.where(named, combine[:, :, None], 0.0), axis=1)
    all_tokens = lax.all_gather(tokens, ("grp", "ex"), axis=0, tiled=True)
    all_coefficient = lax.all_gather(coefficient, ("grp", "ex"), axis=0, tiled=True)
    own_column = jnp.arange(expert_count, dtype=jnp.int32) == own_expert
    weight = jnp.sum(jnp.where(own_column[None, :], all_coefficient, 0.0), axis=1)
    gate_matrix = dequantize(gate_up_weight[0, 0, 0], gate_up_scale[0, 0, 0], is_hot)
    up_matrix = dequantize(gate_up_weight[0, 0, 1], gate_up_scale[0, 0, 1], is_hot)
    down_matrix = dequantize(down_weight[0, 0], down_scale[0, 0], is_hot)
    gate_proj = jnp.dot(all_tokens, gate_matrix, preferred_element_type=jnp.float32)
    up_proj = jnp.dot(all_tokens, up_matrix, preferred_element_type=jnp.float32)
    hidden = (jax.nn.silu(gate_proj) * up_proj).astype(jnp.bfloat16)
    partial_value = jnp.dot(hidden, down_matrix, preferred_element_type=jnp.float32)
    routed = weight[:, None] != 0.0
    scaled = jnp.where(routed, partial_value * weight[:, None], 0.0).astype(jnp.bfloat16)
    lane_sum = lax.psum_scatter(
        scaled.reshape(lax.axis_size("grp"), lane_count, tokens.shape[0], -1),
        "ex",
        scatter_dimension=1,
        tiled=False,
    )
    return lax.psum_scatter(lane_sum, "grp", scatter_dimension=0, tiled=False)


def shards(tokens, expert_ids, *rest):
    group_count = lax.axis_size("grp")
    lane_count = lax.axis_size("ex")
    token_count = tokens.shape[0]
    expert_count = group_count // 2 * lane_count
    route_count = token_count * expert_ids.shape[1]
    capacity = max(2, (5 * route_count + 4 * expert_count - 1) // (4 * expert_count))
    chip_rows = group_count * lane_count // 2 * token_count
    if 2 * expert_count * capacity >= chip_rows:
        return dense_shards(tokens, expert_ids, *rest)
    return routed_shards(tokens, expert_ids, *rest)


def solution(mesh):
    return jax.shard_map(
        shards,
        mesh=mesh,
        in_specs=(
            P(("grp", "ex"), None),
            P(("grp", "ex"), None),
            P(("grp", "ex"), None),
            P(),
            P("grp", "ex", None, None, None),
            P("grp", "ex", None, None, None),
            P("grp", "ex", None, None),
            P("grp", "ex", None, None),
        ),
        out_specs=P(("grp", "ex"), None),
        check_vma=False,
    )
```

```python
import functools

import jax
import jax.numpy as jnp
from jax import lax
from jax.experimental import pallas as pl
from jax.experimental.pallas import tpu as pltpu
from jax.sharding import PartitionSpec as P


def dequantize(weights, scales, is_hot):
    group_count = scales.shape[0]
    shaped = weights.reshape(group_count, weights.shape[0] // group_count, weights.shape[1])
    scaled = (shaped * scales[:, None, :]).reshape(weights.shape).astype(jnp.bfloat16)
    return jnp.where(is_hot, weights, scaled)


def routed_shards(
    tokens, expert_ids, combine, hot_flags, gate_up_weight, gate_up_scale, down_weight, down_scale
):
    group_count = lax.axis_size("grp")
    lane_count = lax.axis_size("ex")
    pair_count = group_count // 2
    token_count = tokens.shape[0]
    model_width = tokens.shape[1]
    top_count = expert_ids.shape[1]
    expert_count = pair_count * lane_count
    route_count = token_count * top_count
    capacity = max(2, (5 * route_count + 4 * expert_count - 1) // (4 * expert_count))
    slot_count = expert_count * capacity
    flat_expert = expert_ids.reshape(route_count)
    route_order = jnp.arange(route_count, dtype=jnp.int32)
    earlier = (flat_expert[None, :] == flat_expert[:, None]) & (
        route_order[None, :] < route_order[:, None]
    )
    route_rank = jnp.sum(earlier, axis=1, dtype=jnp.int32)
    slot_of = flat_expert * capacity + route_rank
    slot_match = slot_of[None, :] == jnp.arange(slot_count, dtype=jnp.int32)[:, None]
    filled = jnp.any(slot_match, axis=1)
    source = jnp.sum(jnp.where(slot_match, route_order[None, :] // top_count, 0), axis=1)
    slot_rows = jnp.where(filled[:, None], tokens[source], jnp.zeros((), tokens.dtype))
    outgoing = slot_rows.reshape(pair_count, lane_count, capacity, model_width)
    own_expert = lax.axis_index("grp") // 2 * lane_count + lax.axis_index("ex")
    is_hot = hot_flags[own_expert] == 1
    gate_matrix = dequantize(gate_up_weight[0, 0, 0], gate_up_scale[0, 0, 0], is_hot)
    up_matrix = dequantize(gate_up_weight[0, 0, 1], gate_up_scale[0, 0, 1], is_hot)
    down_matrix = dequantize(down_weight[0, 0], down_scale[0, 0], is_hot)
    pair_index = flat_expert // lane_count
    lane_index = flat_expert % lane_count
    within = lax.all_to_all(outgoing, "ex", split_axis=1, concat_axis=1, tiled=True)
    doubled = jnp.repeat(within, 2, axis=0)
    arrived_block = lax.all_to_all(doubled, "grp", split_axis=0, concat_axis=0, tiled=True)
    flat_rows = arrived_block.reshape(-1, model_width)
    gate_proj = jnp.dot(flat_rows, gate_matrix, preferred_element_type=jnp.float32)
    up_proj = jnp.dot(flat_rows, up_matrix, preferred_element_type=jnp.float32)
    hidden = (jax.nn.silu(gate_proj) * up_proj).astype(jnp.bfloat16)
    partial_value = jnp.dot(hidden, down_matrix, preferred_element_type=jnp.float32).astype(
        jnp.bfloat16
    )
    across = lax.all_to_all(
        partial_value.reshape(arrived_block.shape), "grp", split_axis=0, concat_axis=0, tiled=True
    )
    returned = lax.all_to_all(across, "ex", split_axis=1, concat_axis=1, tiled=True)
    flat_back = returned.reshape(-1, model_width)
    first_index = (2 * pair_index * lane_count + lane_index) * capacity + route_rank
    second_index = first_index + lane_count * capacity
    both_halves = flat_back[first_index].astype(jnp.float32) + flat_back[second_index].astype(
        jnp.float32
    )
    expert_rows = lax.optimization_barrier(both_halves.astype(jnp.bfloat16)).astype(jnp.float32)
    weighted = expert_rows * combine.reshape(route_count)[:, None]
    return jnp.sum(weighted.reshape(token_count, top_count, model_width), axis=1).astype(
        jnp.bfloat16
    )


def fused_kernel(
    planes,
    experts,
    own_ref,
    gate_up_ref,
    gate_up_scale_ref,
    down_ref,
    down_scale_ref,
    out_ref,
    rows_in,
    parts,
    core_in,
    pair_in,
    last_in,
    plane_in,
    gate_up,
    down,
    hidden,
    load_sem,
    plane_sems,
    spread_sems,
    twin_sems,
    core_sems,
    pair_sems,
    last_sems,
    back_sems,
):
    f32, bf16 = jnp.float32, jnp.bfloat16
    rows, width = out_ref.shape
    half = rows // 2
    units = hidden.shape[1]
    z = lax.axis_index("grp")
    lane = lax.axis_index("ex")
    core = lane % 2
    x = (lane // 2) % 2
    y = lane // 4
    expert = z // 2 * lax.axis_size("ex") + lane
    across_x = {"ex": lane + 2 - 4 * x}
    across_y = {"ex": lane + 4 - 8 * y}
    twin = {"ex": lane + 1 - 2 * core}
    neighbours = [across_x, across_y, twin]
    neighbours += [{"grp": lax.rem(z + step, planes)} for step in range(1, planes)]
    own_rows = pl.ds(pl.multiple_of(core * rows, rows), rows)
    twin_rows = pl.ds(pl.multiple_of((1 - core) * rows, rows), rows)
    half_rows = [pl.ds(pl.multiple_of(core * rows + t * half, half), half) for t in range(2)]

    barrier = pltpu.get_barrier_semaphore()
    for neighbour in neighbours:
        pl.semaphore_signal(
            barrier, inc=1, device_id=neighbour, device_id_type=pl.DeviceIdType.MESH
        )
    pl.semaphore_wait(barrier, len(neighbours))

    pending = []

    def send(source, target, sems, index, device):
        copy = pltpu.make_async_remote_copy(
            src_ref=source,
            dst_ref=target,
            send_sem=sems.at[(0,) + index],
            recv_sem=sems.at[(1,) + index],
            device_id=device,
            device_id_type=pl.DeviceIdType.MESH,
        )
        copy.start()
        pending.append(copy)
        return copy

    own_copy = pltpu.make_async_copy(own_ref, rows_in.at[0, y, x, own_rows], load_sem.at[0])
    own_copy.start()
    loads = [
        pltpu.make_async_copy(gate_up_ref.at[0], gate_up.at[0], load_sem.at[1]),
        pltpu.make_async_copy(gate_up_ref.at[1], gate_up.at[1], load_sem.at[2]),
        pltpu.make_async_copy(down_ref, down, load_sem.at[3]),
    ]
    from_plane = {}
    for k in range(1, planes):
        from_plane[k] = send(
            own_ref,
            rows_in.at[k, y, x, own_rows],
            plane_sems,
            (k,),
            {"grp": lax.rem(z + planes - k, planes)},
        )
    own_copy.wait()
    for load in loads:
        load.start()

    spread = {}

    def first_spread(k):
        if k >= planes:
            return
        if k > 0:
            from_plane[k].wait_recv()
        for t in range(2):
            block = rows_in.at[k, y, x, half_rows[t]]
            first, second = (across_x, across_y) if t == 0 else (across_y, across_x)
            spread[k, t, 0] = send(block, block, spread_sems, (k, t, 0), first)
            spread[k, t, 1] = send(block, block, spread_sems, (k, t, 1), second)

    def second_spread(k):
        if k >= planes:
            return
        for t in range(2):
            spread[k, t, 0].wait_recv()
            if t == 0:
                block, second = rows_in.at[k, y, 1 - x, half_rows[t]], across_y
            else:
                block, second = rows_in.at[k, 1 - y, x, half_rows[t]], across_x
            spread[k, t, 2] = send(block, block, spread_sems, (k, t, 2), second)

    twins = {}

    def to_twin(k):
        if k >= planes:
            return
        for t in range(2):
            spread[k, t, 1].wait_recv()
            spread[k, t, 2].wait_recv()
        block = rows_in.at[k, :, :, own_rows]
        twins[k] = send(block, block, twin_sems, (k,), twin)

    def gate_up_phase(k, part):
        tile = min(units, 256)

        def columns_of(n, carry):
            at = pl.ds(pl.multiple_of(n * tile, tile), tile)
            block = rows_in[k, part, :, :, :width].reshape(hidden.shape[0], width)
            gate = jnp.dot(block, gate_up[0, :, at], preferred_element_type=f32)
            up = jnp.dot(block, gate_up[1, :, at], preferred_element_type=f32)
            hidden[:, at] = (gate / (1.0 + jnp.exp(-gate)) * up).astype(bf16)
            return carry

        lax.fori_loop(0, units // tile, columns_of, 0)

    def down_phase(k, part):
        tile = 512 if width % 512 == 0 else 128
        extra = rows_in[k, part, :, :, width:].reshape(hidden.shape[0], -1).astype(f32)
        column = lax.broadcasted_iota(jnp.int32, extra.shape, 1)
        chosen = (
            (column == expert) | (column == expert + experts) | (column == expert + 2 * experts)
        )
        weight = jnp.sum(jnp.where(chosen, extra, 0.0), axis=1, keepdims=True)

        def columns_of(n, carry):
            at = pl.ds(pl.multiple_of(n * tile, tile), tile)
            value = jnp.dot(hidden[...], down[:, at], preferred_element_type=f32)
            value = jnp.where(weight != 0.0, value * weight, 0.0).astype(bf16)
            parts[k, part, :, :, at] = value.reshape(2, 2 * rows, tile)
            return carry

        lax.fori_loop(0, width // tile, columns_of, 0)

    step = 16

    def add_rows(count, target, source):
        def one(i, carry):
            at_target, at_source = target(i), source(i)
            total = parts[at_target].astype(f32) + at_source[0][at_source[1]].astype(f32)
            parts[at_target] = total.astype(bf16)
            return carry

        lax.fori_loop(0, count, one, 0)

    returns = {}

    def return_core(k):
        returns[k, "core"] = send(
            parts.at[k, :, :, twin_rows], core_in.at[k], core_sems, (k,), twin
        )

    def return_pair(k):
        if k < 0:
            return
        returns[k, "core"].wait_recv()
        per = rows // step

        def target(i):
            at = pl.ds(pl.multiple_of(core * rows + i % per * step, step), step)
            return (k, i // per // 2, i // per % 2, at)

        def source(i):
            at = pl.ds(pl.multiple_of(i % per * step, step), step)
            return core_in, (k, i // per // 2, i // per % 2, at)

        add_rows(4 * per, target, source)
        returns[k, "a"] = send(
            parts.at[k, 1 - y, :, half_rows[0]], pair_in.at[k, 0], pair_sems, (k, 0), across_y
        )
        returns[k, "b"] = send(
            parts.at[k, :, 1 - x, half_rows[1]], pair_in.at[k, 1], pair_sems, (k, 1), across_x
        )

    def return_last(k):
        if k < 0:
            return
        per = half // step
        for t in range(2):
            returns[k, "ab"[t]].wait_recv()

            def target(i, t=t):
                at = pl.ds(pl.multiple_of(core * rows + t * half + i % per * step, step), step)
                return (k, y, i // per, at) if t == 0 else (k, i // per, x, at)

            def source(i, t=t):
                at = pl.ds(pl.multiple_of(i % per * step, step), step)
                return pair_in, (k, t, i // per, at)

            add_rows(2 * per, target, source)
        returns[k, "c"] = send(
            parts.at[k, y, 1 - x, half_rows[0]], last_in.at[k, 0], last_sems, (k, 0), across_x
        )
        returns[k, "d"] = send(
            parts.at[k, 1 - y, x, half_rows[1]], last_in.at[k, 1], last_sems, (k, 1), across_y
        )

    def return_plane(k):
        if k < 0:
            return
        per = half // step
        for t in range(2):
            returns[k, "cd"[t]].wait_recv()

            def target(i, t=t):
                at = pl.ds(pl.multiple_of(core * rows + t * half + i * step, step), step)
                return (k, y, x, at)

            def source(i, t=t):
                at = pl.ds(pl.multiple_of(i * step, step), step)
                return last_in, (k, t, at)

            add_rows(per, target, source)
        if k > 0:
            returns[k, "z"] = send(
                parts.at[k, y, x, own_rows],
                plane_in.at[k],
                back_sems,
                (k,),
                {"grp": lax.rem(z + k, planes)},
            )

    def scale_rows(ref, scales, pick):
        groups = scales.shape[0]
        size = ref.shape[0] // groups

        def one(g, carry):
            at = pl.ds(pl.multiple_of(g * size, size), size)
            ref[at] = (ref[at].astype(f32) * scales[pl.ds(g, 1), :]).astype(bf16)
            return carry

        lax.fori_loop(0, groups, one, 0)

    first_spread(0)
    loads[0].wait()
    scale_rows(gate_up.at[0], gate_up_scale_ref.at[0], 0)
    second_spread(0)
    first_spread(1)
    loads[1].wait()
    scale_rows(gate_up.at[1], gate_up_scale_ref.at[1], 0)
    loads[2].wait()
    scale_rows(down, down_scale_ref, 0)
    to_twin(0)

    for k in range(planes):
        second_spread(k + 1)
        first_spread(k + 2)
        twins[k].wait_recv()
        gate_up_phase(k, 0)
        return_pair(k - 1)
        down_phase(k, 0)
        return_last(k - 1)
        gate_up_phase(k, 1)
        down_phase(k, 1)
        return_plane(k - 1)
        to_twin(k + 1)
        return_core(k)
    return_pair(planes - 1)
    return_last(planes - 1)
    return_plane(planes - 1)
    for k in range(1, planes):
        returns[k, "z"].wait_recv()

    def finish(i, carry):
        at = pl.ds(pl.multiple_of(i * step, step), step)
        mine = pl.ds(pl.multiple_of(core * rows + i * step, step), step)
        total = parts[0, y, x, mine].astype(f32)
        for k in range(1, planes):
            total = total + plane_in[k, at].astype(f32)
        out_ref[at] = total.astype(bf16)
        return carry

    lax.fori_loop(0, rows // step, finish, 0)
    for copy in pending:
        copy.wait_send()


def dense_shards(
    tokens, expert_ids, combine, hot_flags, gate_up_weight, gate_up_scale, down_weight, down_scale
):
    planes = lax.axis_size("grp")
    lane_count = lax.axis_size("ex")
    expert_count = planes // 2 * lane_count
    rows, width = tokens.shape
    units = down_weight.shape[2]
    own_expert = lax.axis_index("grp") // 2 * lane_count + lax.axis_index("ex")
    is_hot = hot_flags[own_expert] == 1
    named = expert_ids[:, :, None] == jnp.arange(expert_count, dtype=jnp.int32)
    coefficient = jnp.sum(jnp.where(named, combine[:, :, None], 0.0), axis=1)
    pieces, rest = [], coefficient
    for _ in range(3):
        piece = lax.reduce_precision(rest, 8, 7)
        pieces.append(piece.astype(jnp.bfloat16))
        rest = rest - piece
    extra = -(-3 * expert_count // 128) * 128
    blank = jnp.zeros((rows, extra - 3 * expert_count), jnp.bfloat16)
    own_rows = jnp.concatenate([tokens] + pieces + [blank], axis=1)
    gate_up_factor = jnp.where(is_hot, 1.0, gate_up_scale[0, 0])
    down_factor = jnp.where(is_hot, 1.0, down_scale[0, 0])
    bf16 = jnp.bfloat16
    dma = pltpu.SemaphoreType.DMA
    return pl.pallas_call(
        functools.partial(fused_kernel, planes, expert_count),
        out_shape=jax.ShapeDtypeStruct((rows, width), bf16),
        in_specs=[
            pl.BlockSpec(memory_space=pl.ANY),
            pl.BlockSpec(memory_space=pl.ANY),
            pl.BlockSpec(memory_space=pltpu.VMEM),
            pl.BlockSpec(memory_space=pl.ANY),
            pl.BlockSpec(memory_space=pltpu.VMEM),
        ],
        out_specs=pl.BlockSpec(memory_space=pltpu.VMEM),
        scratch_shapes=[
            pltpu.VMEM((planes, 2, 2, 2 * rows, width + extra), bf16),
            pltpu.VMEM((planes, 2, 2, 2 * rows, width), bf16),
            pltpu.VMEM((planes, 2, 2, rows, width), bf16),
            pltpu.VMEM((planes, 2, 2, rows // 2, width), bf16),
            pltpu.VMEM((planes, 2, rows // 2, width), bf16),
            pltpu.VMEM((planes, rows, width), bf16),
            pltpu.VMEM((2, width, units), bf16),
            pltpu.VMEM((units, width), bf16),
            pltpu.VMEM((4 * rows, units), bf16),
            dma((4,)),
            dma((2, planes)),
            dma((2, planes, 2, 3)),
            dma((2, planes)),
            dma((2, planes)),
            dma((2, planes, 2)),
            dma((2, planes, 2)),
            dma((2, planes)),
        ],
        compiler_params=pltpu.CompilerParams(
            collective_id=0, has_side_effects=True, vmem_limit_bytes=67043328
        ),
    )(own_rows, gate_up_weight[0, 0], gate_up_factor, down_weight[0, 0], down_factor)


def shards(tokens, expert_ids, *rest):
    group_count = lax.axis_size("grp")
    lane_count = lax.axis_size("ex")
    token_count = tokens.shape[0]
    expert_count = group_count // 2 * lane_count
    route_count = token_count * expert_ids.shape[1]
    capacity = max(2, (5 * route_count + 4 * expert_count - 1) // (4 * expert_count))
    chip_rows = group_count * lane_count // 2 * token_count
    if lane_count == 2 * 2 * 2 and 2 * expert_count * capacity >= chip_rows:
        return dense_shards(tokens, expert_ids, *rest)
    return routed_shards(tokens, expert_ids, *rest)


def solution(mesh):
    return jax.shard_map(
        shards,
        mesh=mesh,
        in_specs=(
            P(("grp", "ex"), None),
            P(("grp", "ex"), None),
            P(("grp", "ex"), None),
            P(),
            P("grp", "ex", None, None, None),
            P("grp", "ex", None, None, None),
            P("grp", "ex", None, None),
            P("grp", "ex", None, None),
        ),
        out_specs=P(("grp", "ex"), None),
        check_vma=False,
    )
```

```python
import functools

import jax
import jax.numpy as jnp
from jax import lax
from jax.experimental import pallas as pl
from jax.experimental.pallas import tpu as pltpu
from jax.sharding import PartitionSpec as P


def dequantize(weights, scales, is_hot):
    group_count = scales.shape[0]
    shaped = weights.reshape(group_count, weights.shape[0] // group_count, weights.shape[1])
    scaled = (shaped * scales[:, None, :]).reshape(weights.shape).astype(jnp.bfloat16)
    return jnp.where(is_hot, weights, scaled)


def routed_shards(
    tokens, expert_ids, combine, hot_flags, gate_up_weight, gate_up_scale, down_weight, down_scale
):
    group_count = lax.axis_size("grp")
    lane_count = lax.axis_size("ex")
    pair_count = group_count // 2
    token_count = tokens.shape[0]
    model_width = tokens.shape[1]
    top_count = expert_ids.shape[1]
    expert_count = pair_count * lane_count
    route_count = token_count * top_count
    capacity = max(2, (5 * route_count + 4 * expert_count - 1) // (4 * expert_count))
    slot_count = expert_count * capacity
    flat_expert = expert_ids.reshape(route_count)
    route_order = jnp.arange(route_count, dtype=jnp.int32)
    earlier = (flat_expert[None, :] == flat_expert[:, None]) & (
        route_order[None, :] < route_order[:, None]
    )
    route_rank = jnp.sum(earlier, axis=1, dtype=jnp.int32)
    slot_of = flat_expert * capacity + route_rank
    slot_match = slot_of[None, :] == jnp.arange(slot_count, dtype=jnp.int32)[:, None]
    filled = jnp.any(slot_match, axis=1)
    source = jnp.sum(jnp.where(slot_match, route_order[None, :] // top_count, 0), axis=1)
    slot_rows = jnp.where(filled[:, None], tokens[source], jnp.zeros((), tokens.dtype))
    outgoing = slot_rows.reshape(pair_count, lane_count, capacity, model_width)
    own_expert = lax.axis_index("grp") // 2 * lane_count + lax.axis_index("ex")
    is_hot = hot_flags[own_expert] == 1
    gate_matrix = dequantize(gate_up_weight[0, 0, 0], gate_up_scale[0, 0, 0], is_hot)
    up_matrix = dequantize(gate_up_weight[0, 0, 1], gate_up_scale[0, 0, 1], is_hot)
    down_matrix = dequantize(down_weight[0, 0], down_scale[0, 0], is_hot)
    pair_index = flat_expert // lane_count
    lane_index = flat_expert % lane_count
    within = lax.all_to_all(outgoing, "ex", split_axis=1, concat_axis=1, tiled=True)
    doubled = jnp.repeat(within, 2, axis=0)
    arrived_block = lax.all_to_all(doubled, "grp", split_axis=0, concat_axis=0, tiled=True)
    flat_rows = arrived_block.reshape(-1, model_width)
    gate_proj = jnp.dot(flat_rows, gate_matrix, preferred_element_type=jnp.float32)
    up_proj = jnp.dot(flat_rows, up_matrix, preferred_element_type=jnp.float32)
    hidden = (jax.nn.silu(gate_proj) * up_proj).astype(jnp.bfloat16)
    partial_value = jnp.dot(hidden, down_matrix, preferred_element_type=jnp.float32).astype(
        jnp.bfloat16
    )
    across = lax.all_to_all(
        partial_value.reshape(arrived_block.shape), "grp", split_axis=0, concat_axis=0, tiled=True
    )
    returned = lax.all_to_all(across, "ex", split_axis=1, concat_axis=1, tiled=True)
    flat_back = returned.reshape(-1, model_width)
    first_index = (2 * pair_index * lane_count + lane_index) * capacity + route_rank
    second_index = first_index + lane_count * capacity
    both_halves = flat_back[first_index].astype(jnp.float32) + flat_back[second_index].astype(
        jnp.float32
    )
    expert_rows = lax.optimization_barrier(both_halves.astype(jnp.bfloat16)).astype(jnp.float32)
    weighted = expert_rows * combine.reshape(route_count)[:, None]
    return jnp.sum(weighted.reshape(token_count, top_count, model_width), axis=1).astype(
        jnp.bfloat16
    )


def fused_kernel(
    planes,
    experts,
    own_ref,
    gate_up_ref,
    gate_up_scale_ref,
    down_ref,
    down_scale_ref,
    out_ref,
    rows_in,
    parts,
    core_in,
    pair_in,
    last_in,
    plane_in,
    gate_up,
    down,
    hidden,
    load_sem,
    plane_sems,
    spread_sems,
    twin_sems,
    core_sems,
    pair_sems,
    last_sems,
    back_sems,
):
    f32, bf16 = jnp.float32, jnp.bfloat16
    rows, width = out_ref.shape
    half = rows // 2
    units = hidden.shape[1]
    z = lax.axis_index("grp")
    lane = lax.axis_index("ex")
    core = lane % 2
    x = (lane // 2) % 2
    y = lane // 4
    expert = z // 2 * lax.axis_size("ex") + lane
    across_x = {"ex": lane + 2 - 4 * x}
    across_y = {"ex": lane + 4 - 8 * y}
    twin = {"ex": lane + 1 - 2 * core}
    neighbours = [across_x, across_y, twin]
    neighbours += [{"grp": lax.rem(z + step, planes)} for step in range(1, planes)]
    own_rows = pl.ds(pl.multiple_of(core * rows, rows), rows)
    twin_rows = pl.ds(pl.multiple_of((1 - core) * rows, rows), rows)
    half_rows = [pl.ds(pl.multiple_of(core * rows + t * half, half), half) for t in range(2)]

    barrier = pltpu.get_barrier_semaphore()
    for neighbour in neighbours:
        pl.semaphore_signal(
            barrier, inc=1, device_id=neighbour, device_id_type=pl.DeviceIdType.MESH
        )
    pl.semaphore_wait(barrier, len(neighbours))

    pending = []

    def send(source, target, sems, index, device):
        copy = pltpu.make_async_remote_copy(
            src_ref=source,
            dst_ref=target,
            send_sem=sems.at[(0,) + index],
            recv_sem=sems.at[(1,) + index],
            device_id=device,
            device_id_type=pl.DeviceIdType.MESH,
        )
        copy.start()
        pending.append(copy)
        return copy

    own_copy = pltpu.make_async_copy(own_ref, rows_in.at[0, y, x, own_rows], load_sem.at[0])
    own_copy.start()
    loads = [
        pltpu.make_async_copy(gate_up_ref.at[0], gate_up.at[0], load_sem.at[1]),
        pltpu.make_async_copy(gate_up_ref.at[1], gate_up.at[1], load_sem.at[2]),
        pltpu.make_async_copy(down_ref, down, load_sem.at[3]),
    ]
    from_plane = {}

    def to_plane(k):
        if k >= planes:
            return
        from_plane[k] = send(
            own_ref,
            rows_in.at[k, y, x, own_rows],
            plane_sems,
            (k,),
            {"grp": lax.rem(z + planes - k, planes)},
        )

    to_plane(1)
    to_plane(2)
    own_copy.wait()
    for load in loads:
        load.start()

    spread = {}

    def first_spread(k):
        if k >= planes:
            return
        if k > 0:
            from_plane[k].wait_recv()
        for t in range(2):
            block = rows_in.at[k, y, x, half_rows[t]]
            first, second = (across_x, across_y) if t == 0 else (across_y, across_x)
            spread[k, t, 0] = send(block, block, spread_sems, (k, t, 0), first)
            spread[k, t, 1] = send(block, block, spread_sems, (k, t, 1), second)

    def second_spread(k):
        if k >= planes:
            return
        for t in range(2):
            spread[k, t, 0].wait_recv()
            if t == 0:
                block, second = rows_in.at[k, y, 1 - x, half_rows[t]], across_y
            else:
                block, second = rows_in.at[k, 1 - y, x, half_rows[t]], across_x
            spread[k, t, 2] = send(block, block, spread_sems, (k, t, 2), second)

    twins = {}

    def to_twin(k):
        if k >= planes:
            return
        for t in range(2):
            spread[k, t, 1].wait_recv()
            spread[k, t, 2].wait_recv()
        block = rows_in.at[k, :, :, own_rows]
        twins[k] = send(block, block, twin_sems, (k,), twin)

    def gate_up_phase(k, part):
        tile = min(units, 256)

        def columns_of(n, carry):
            at = pl.ds(pl.multiple_of(n * tile, tile), tile)
            block = rows_in[k, part, :, :, :width].reshape(hidden.shape[0], width)
            gate = jnp.dot(block, gate_up[0, :, at], preferred_element_type=f32)
            up = jnp.dot(block, gate_up[1, :, at], preferred_element_type=f32)
            hidden[:, at] = (gate / (1.0 + jnp.exp(-gate)) * up).astype(bf16)
            return carry

        lax.fori_loop(0, units // tile, columns_of, 0)

    def down_phase(k, part):
        tile = 512 if width % 512 == 0 else 128
        extra = rows_in[k, part, :, :, width:].reshape(hidden.shape[0], -1).astype(f32)
        column = lax.broadcasted_iota(jnp.int32, extra.shape, 1)
        chosen = (
            (column == expert) | (column == expert + experts) | (column == expert + 2 * experts)
        )
        weight = jnp.sum(jnp.where(chosen, extra, 0.0), axis=1, keepdims=True)

        def columns_of(n, carry):
            at = pl.ds(pl.multiple_of(n * tile, tile), tile)
            value = jnp.dot(hidden[...], down[:, at], preferred_element_type=f32)
            value = jnp.where(weight != 0.0, value * weight, 0.0).astype(bf16)
            parts[k, part, :, :, at] = value.reshape(2, 2 * rows, tile)
            return carry

        lax.fori_loop(0, width // tile, columns_of, 0)

    step = 16

    def add_rows(count, target, source):
        def one(i, carry):
            at_target, at_source = target(i), source(i)
            total = parts[at_target].astype(f32) + at_source[0][at_source[1]].astype(f32)
            parts[at_target] = total.astype(bf16)
            return carry

        lax.fori_loop(0, count, one, 0)

    returns = {}

    def return_core(k):
        returns[k, "core"] = send(
            parts.at[k, :, :, twin_rows], core_in.at[k], core_sems, (k,), twin
        )

    def return_pair(k):
        if k < 0:
            return
        returns[k, "core"].wait_recv()
        per = rows // step

        def target(i):
            at = pl.ds(pl.multiple_of(core * rows + i % per * step, step), step)
            return (k, i // per // 2, i // per % 2, at)

        def source(i):
            at = pl.ds(pl.multiple_of(i % per * step, step), step)
            return core_in, (k, i // per // 2, i // per % 2, at)

        add_rows(4 * per, target, source)
        returns[k, "a"] = send(
            parts.at[k, 1 - y, :, half_rows[0]], pair_in.at[k, 0], pair_sems, (k, 0), across_y
        )
        returns[k, "b"] = send(
            parts.at[k, :, 1 - x, half_rows[1]], pair_in.at[k, 1], pair_sems, (k, 1), across_x
        )

    def return_last(k):
        if k < 0:
            return
        per = half // step
        for t in range(2):
            returns[k, "ab"[t]].wait_recv()

            def target(i, t=t):
                at = pl.ds(pl.multiple_of(core * rows + t * half + i % per * step, step), step)
                return (k, y, i // per, at) if t == 0 else (k, i // per, x, at)

            def source(i, t=t):
                at = pl.ds(pl.multiple_of(i % per * step, step), step)
                return pair_in, (k, t, i // per, at)

            add_rows(2 * per, target, source)
        returns[k, "c"] = send(
            parts.at[k, y, 1 - x, half_rows[0]], last_in.at[k, 0], last_sems, (k, 0), across_x
        )
        returns[k, "d"] = send(
            parts.at[k, 1 - y, x, half_rows[1]], last_in.at[k, 1], last_sems, (k, 1), across_y
        )

    def return_plane(k):
        if k < 0:
            return
        per = half // step
        for t in range(2):
            returns[k, "cd"[t]].wait_recv()

            def target(i, t=t):
                at = pl.ds(pl.multiple_of(core * rows + t * half + i * step, step), step)
                return (k, y, x, at)

            def source(i, t=t):
                at = pl.ds(pl.multiple_of(i * step, step), step)
                return last_in, (k, t, at)

            add_rows(per, target, source)
        if k > 0:
            returns[k, "z"] = send(
                parts.at[k, y, x, own_rows],
                plane_in.at[k],
                back_sems,
                (k,),
                {"grp": lax.rem(z + k, planes)},
            )

    def scale_rows(ref, scales):
        groups = scales.shape[0]
        size = ref.shape[0] // groups

        def one(g, carry):
            at = pl.ds(pl.multiple_of(g * size, size), size)
            ref[at] = (ref[at].astype(f32) * scales[pl.ds(g, 1), :]).astype(bf16)
            return carry

        lax.fori_loop(0, groups, one, 0)

    first_spread(0)
    loads[0].wait()
    scale_rows(gate_up.at[0], gate_up_scale_ref.at[0])
    second_spread(0)
    first_spread(1)
    loads[1].wait()
    scale_rows(gate_up.at[1], gate_up_scale_ref.at[1])
    loads[2].wait()
    scale_rows(down, down_scale_ref)
    to_twin(0)
    second_spread(1)

    for k in range(planes):
        for later in range(k + 3, planes if k == 0 else k + 3):
            to_plane(later)
        first_spread(k + 2)
        if k > 2:
            return_pair(k - 1)
        twins[k].wait_recv()
        gate_up_phase(k, 0)
        down_phase(k, 0)
        to_twin(k + 1)
        second_spread(k + 2)
        if k == planes - 1:
            return_pair(0)
            return_last(1)
        gate_up_phase(k, 1)
        down_phase(k, 1)
        return_core(k)
        if k == 2:
            return_pair(1)
    return_pair(planes - 1)
    for k in range(2, planes):
        return_last(k)
        return_plane(k - 1)
    return_last(0)
    return_plane(planes - 1)
    return_plane(0)
    for k in range(1, planes):
        returns[k, "z"].wait_recv()

    def finish(i, carry):
        at = pl.ds(pl.multiple_of(i * step, step), step)
        mine = pl.ds(pl.multiple_of(core * rows + i * step, step), step)
        total = parts[0, y, x, mine].astype(f32)
        for k in range(1, planes):
            total = total + plane_in[k, at].astype(f32)
        out_ref[at] = total.astype(bf16)
        return carry

    lax.fori_loop(0, rows // step, finish, 0)
    for copy in pending:
        copy.wait_send()


def dense_shards(
    tokens, expert_ids, combine, hot_flags, gate_up_weight, gate_up_scale, down_weight, down_scale
):
    planes = lax.axis_size("grp")
    lane_count = lax.axis_size("ex")
    expert_count = planes // 2 * lane_count
    rows, width = tokens.shape
    units = down_weight.shape[2]
    own_expert = lax.axis_index("grp") // 2 * lane_count + lax.axis_index("ex")
    is_hot = hot_flags[own_expert] == 1
    named = expert_ids[:, :, None] == jnp.arange(expert_count, dtype=jnp.int32)
    coefficient = jnp.sum(jnp.where(named, combine[:, :, None], 0.0), axis=1)
    pieces, rest = [], coefficient
    for _ in range(3):
        piece = lax.reduce_precision(rest, 8, 7)
        pieces.append(piece.astype(jnp.bfloat16))
        rest = rest - piece
    extra = -(-3 * expert_count // 128) * 128
    blank = jnp.zeros((rows, extra - 3 * expert_count), jnp.bfloat16)
    own_rows = jnp.concatenate([tokens] + pieces + [blank], axis=1)
    gate_up_factor = jnp.where(is_hot, 1.0, gate_up_scale[0, 0])
    down_factor = jnp.where(is_hot, 1.0, down_scale[0, 0])
    bf16 = jnp.bfloat16
    dma = pltpu.SemaphoreType.DMA
    return pl.pallas_call(
        functools.partial(fused_kernel, planes, expert_count),
        out_shape=jax.ShapeDtypeStruct((rows, width), bf16),
        in_specs=[
            pl.BlockSpec(memory_space=pl.ANY),
            pl.BlockSpec(memory_space=pl.ANY),
            pl.BlockSpec(memory_space=pltpu.VMEM),
            pl.BlockSpec(memory_space=pl.ANY),
            pl.BlockSpec(memory_space=pltpu.VMEM),
        ],
        out_specs=pl.BlockSpec(memory_space=pltpu.VMEM),
        scratch_shapes=[
            pltpu.VMEM((planes, 2, 2, 2 * rows, width + extra), bf16),
            pltpu.VMEM((planes, 2, 2, 2 * rows, width), bf16),
            pltpu.VMEM((planes, 2, 2, rows, width), bf16),
            pltpu.VMEM((planes, 2, 2, rows // 2, width), bf16),
            pltpu.VMEM((planes, 2, rows // 2, width), bf16),
            pltpu.VMEM((planes, rows, width), bf16),
            pltpu.VMEM((2, width, units), bf16),
            pltpu.VMEM((units, width), bf16),
            pltpu.VMEM((4 * rows, units), bf16),
            dma((4,)),
            dma((2, planes)),
            dma((2, planes, 2, 3)),
            dma((2, planes)),
            dma((2, planes)),
            dma((2, planes, 2)),
            dma((2, planes, 2)),
            dma((2, planes)),
        ],
        compiler_params=pltpu.CompilerParams(
            collective_id=0, has_side_effects=True, vmem_limit_bytes=67043328
        ),
    )(own_rows, gate_up_weight[0, 0], gate_up_factor, down_weight[0, 0], down_factor)


def shards(tokens, expert_ids, *rest):
    group_count = lax.axis_size("grp")
    lane_count = lax.axis_size("ex")
    token_count = tokens.shape[0]
    expert_count = group_count // 2 * lane_count
    route_count = token_count * expert_ids.shape[1]
    capacity = max(2, (5 * route_count + 4 * expert_count - 1) // (4 * expert_count))
    chip_rows = group_count * lane_count // 2 * token_count
    if lane_count == 2 * 2 * 2 and 2 * expert_count * capacity >= chip_rows:
        return dense_shards(tokens, expert_ids, *rest)
    return routed_shards(tokens, expert_ids, *rest)


def solution(mesh):
    return jax.shard_map(
        shards,
        mesh=mesh,
        in_specs=(
            P(("grp", "ex"), None),
            P(("grp", "ex"), None),
            P(("grp", "ex"), None),
            P(),
            P("grp", "ex", None, None, None),
            P("grp", "ex", None, None, None),
            P("grp", "ex", None, None),
            P("grp", "ex", None, None),
        ),
        out_specs=P(("grp", "ex"), None),
        check_vma=False,
    )
```

```python
import functools

import jax
import jax.numpy as jnp
from jax import lax
from jax.experimental import pallas as pl
from jax.experimental.pallas import tpu as pltpu
from jax.sharding import PartitionSpec as P


def dequantize(weights, scales, is_hot):
    group_count = scales.shape[0]
    shaped = weights.reshape(group_count, weights.shape[0] // group_count, weights.shape[1])
    scaled = (shaped * scales[:, None, :]).reshape(weights.shape).astype(jnp.bfloat16)
    return jnp.where(is_hot, weights, scaled)


def routed_shards(
    tokens, expert_ids, combine, hot_flags, gate_up_weight, gate_up_scale, down_weight, down_scale
):
    group_count = lax.axis_size("grp")
    lane_count = lax.axis_size("ex")
    pair_count = group_count // 2
    token_count = tokens.shape[0]
    model_width = tokens.shape[1]
    top_count = expert_ids.shape[1]
    expert_count = pair_count * lane_count
    route_count = token_count * top_count
    capacity = max(2, (5 * route_count + 4 * expert_count - 1) // (4 * expert_count))
    slot_count = expert_count * capacity
    flat_expert = expert_ids.reshape(route_count)
    route_order = jnp.arange(route_count, dtype=jnp.int32)
    earlier = (flat_expert[None, :] == flat_expert[:, None]) & (
        route_order[None, :] < route_order[:, None]
    )
    route_rank = jnp.sum(earlier, axis=1, dtype=jnp.int32)
    slot_of = flat_expert * capacity + route_rank
    slot_match = slot_of[None, :] == jnp.arange(slot_count, dtype=jnp.int32)[:, None]
    filled = jnp.any(slot_match, axis=1)
    source = jnp.sum(jnp.where(slot_match, route_order[None, :] // top_count, 0), axis=1)
    slot_rows = jnp.where(filled[:, None], tokens[source], jnp.zeros((), tokens.dtype))
    outgoing = slot_rows.reshape(pair_count, lane_count, capacity, model_width)
    own_expert = lax.axis_index("grp") // 2 * lane_count + lax.axis_index("ex")
    is_hot = hot_flags[own_expert] == 1
    gate_matrix = dequantize(gate_up_weight[0, 0, 0], gate_up_scale[0, 0, 0], is_hot)
    up_matrix = dequantize(gate_up_weight[0, 0, 1], gate_up_scale[0, 0, 1], is_hot)
    down_matrix = dequantize(down_weight[0, 0], down_scale[0, 0], is_hot)
    pair_index = flat_expert // lane_count
    lane_index = flat_expert % lane_count
    within = lax.all_to_all(outgoing, "ex", split_axis=1, concat_axis=1, tiled=True)
    doubled = jnp.repeat(within, 2, axis=0)
    arrived_block = lax.all_to_all(doubled, "grp", split_axis=0, concat_axis=0, tiled=True)
    flat_rows = arrived_block.reshape(-1, model_width)
    gate_proj = jnp.dot(flat_rows, gate_matrix, preferred_element_type=jnp.float32)
    up_proj = jnp.dot(flat_rows, up_matrix, preferred_element_type=jnp.float32)
    hidden = (jax.nn.silu(gate_proj) * up_proj).astype(jnp.bfloat16)
    partial_value = jnp.dot(hidden, down_matrix, preferred_element_type=jnp.float32).astype(
        jnp.bfloat16
    )
    across = lax.all_to_all(
        partial_value.reshape(arrived_block.shape), "grp", split_axis=0, concat_axis=0, tiled=True
    )
    returned = lax.all_to_all(across, "ex", split_axis=1, concat_axis=1, tiled=True)
    flat_back = returned.reshape(-1, model_width)
    first_index = (2 * pair_index * lane_count + lane_index) * capacity + route_rank
    second_index = first_index + lane_count * capacity
    both_halves = flat_back[first_index].astype(jnp.float32) + flat_back[second_index].astype(
        jnp.float32
    )
    expert_rows = lax.optimization_barrier(both_halves.astype(jnp.bfloat16)).astype(jnp.float32)
    weighted = expert_rows * combine.reshape(route_count)[:, None]
    return jnp.sum(weighted.reshape(token_count, top_count, model_width), axis=1).astype(
        jnp.bfloat16
    )


def fused_kernel(
    planes,
    experts,
    hot_ref,
    own_ref,
    gate_up_ref,
    gate_up_scale_ref,
    down_ref,
    down_scale_ref,
    out_ref,
    rows_in,
    parts,
    core_in,
    pair_in,
    last_in,
    plane_in,
    gate_up,
    down,
    hidden,
    load_sem,
    plane_sems,
    spread_sems,
    twin_sems,
    core_sems,
    pair_sems,
    last_sems,
    back_sems,
):
    f32, bf16 = jnp.float32, jnp.bfloat16
    rows, width = out_ref.shape
    half = rows // 2
    units = hidden.shape[1]
    z = lax.axis_index("grp")
    lane = lax.axis_index("ex")
    core = lane % 2
    x = (lane // 2) % 2
    y = lane // 4
    expert = z // 2 * lax.axis_size("ex") + lane
    across_x = {"ex": lane + 2 - 4 * x}
    across_y = {"ex": lane + 4 - 8 * y}
    twin = {"ex": lane + 1 - 2 * core}
    neighbours = [across_x, across_y, twin]
    neighbours += [{"grp": lax.rem(z + step, planes)} for step in range(1, planes)]
    is_hot = hot_ref[expert] == 1
    own_rows = pl.ds(pl.multiple_of(core * rows, rows), rows)
    twin_rows = pl.ds(pl.multiple_of((1 - core) * rows, rows), rows)
    half_rows = [pl.ds(pl.multiple_of(core * rows + t * half, half), half) for t in range(2)]

    barrier = pltpu.get_barrier_semaphore()
    for neighbour in neighbours:
        pl.semaphore_signal(
            barrier, inc=1, device_id=neighbour, device_id_type=pl.DeviceIdType.MESH
        )
    pl.semaphore_wait(barrier, len(neighbours))

    pending = []

    def send(source, target, sems, index, device):
        copy = pltpu.make_async_remote_copy(
            src_ref=source,
            dst_ref=target,
            send_sem=sems.at[(0,) + index],
            recv_sem=sems.at[(1,) + index],
            device_id=device,
            device_id_type=pl.DeviceIdType.MESH,
        )
        copy.start()
        pending.append(copy)
        return copy

    own_copy = pltpu.make_async_copy(own_ref, rows_in.at[0, y, x, own_rows], load_sem.at[0])
    own_copy.start()
    loads = [
        pltpu.make_async_copy(gate_up_ref.at[0], gate_up.at[0], load_sem.at[1]),
        pltpu.make_async_copy(gate_up_ref.at[1], gate_up.at[1], load_sem.at[2]),
        pltpu.make_async_copy(down_ref, down, load_sem.at[3]),
    ]
    from_plane = {}

    def to_plane(k):
        if k >= planes:
            return
        from_plane[k] = send(
            own_ref,
            rows_in.at[k, y, x, own_rows],
            plane_sems,
            (k,),
            {"grp": lax.rem(z + planes - k, planes)},
        )

    to_plane(1)
    to_plane(2)
    own_copy.wait()
    for load in loads:
        load.start()

    spread = {}

    def first_spread(k):
        if k >= planes:
            return
        if k > 0:
            from_plane[k].wait_recv()
        for t in range(2):
            block = rows_in.at[k, y, x, half_rows[t]]
            first, second = (across_x, across_y) if t == 0 else (across_y, across_x)
            spread[k, t, 0] = send(block, block, spread_sems, (k, t, 0), first)
            spread[k, t, 1] = send(block, block, spread_sems, (k, t, 1), second)

    def second_spread(k):
        if k >= planes:
            return
        for t in range(2):
            spread[k, t, 0].wait_recv()
            if t == 0:
                block, second = rows_in.at[k, y, 1 - x, half_rows[t]], across_y
            else:
                block, second = rows_in.at[k, 1 - y, x, half_rows[t]], across_x
            spread[k, t, 2] = send(block, block, spread_sems, (k, t, 2), second)

    twins = {}

    def to_twin(k):
        if k >= planes:
            return
        for t in range(2):
            spread[k, t, 1].wait_recv()
            spread[k, t, 2].wait_recv()
        block = rows_in.at[k, :, :, own_rows]
        twins[k] = send(block, block, twin_sems, (k,), twin)

    def gate_up_phase(k, part):
        tile = min(units, 256)

        def columns_of(n, carry):
            at = pl.ds(pl.multiple_of(n * tile, tile), tile)
            block = rows_in[k, part, :, :, :width].reshape(hidden.shape[0], width)
            gate = jnp.dot(block, gate_up[0, :, at], preferred_element_type=f32)
            up = jnp.dot(block, gate_up[1, :, at], preferred_element_type=f32)
            hidden[:, at] = (gate / (1.0 + jnp.exp(-gate)) * up).astype(bf16)
            return carry

        lax.fori_loop(0, units // tile, columns_of, 0)

    def down_phase(k, part):
        tile = 512 if width % 512 == 0 else 128
        extra = rows_in[k, part, :, :, width:].reshape(hidden.shape[0], -1).astype(f32)
        column = lax.broadcasted_iota(jnp.int32, extra.shape, 1)
        chosen = (
            (column == expert) | (column == expert + experts) | (column == expert + 2 * experts)
        )
        weight = jnp.sum(jnp.where(chosen, extra, 0.0), axis=1, keepdims=True)

        def columns_of(n, carry):
            at = pl.ds(pl.multiple_of(n * tile, tile), tile)
            value = jnp.dot(hidden[...], down[:, at], preferred_element_type=f32)
            value = jnp.where(weight != 0.0, value * weight, 0.0).astype(bf16)
            parts[k, part, :, :, at] = value.reshape(2, 2 * rows, tile)
            return carry

        lax.fori_loop(0, width // tile, columns_of, 0)

    step = 16

    def add_rows(count, target, source):
        def one(i, carry):
            at_target, at_source = target(i), source(i)
            total = parts[at_target].astype(f32) + at_source[0][at_source[1]].astype(f32)
            parts[at_target] = total.astype(bf16)
            return carry

        lax.fori_loop(0, count, one, 0)

    returns = {}

    def return_core(k):
        returns[k, "core"] = send(
            parts.at[k, :, :, twin_rows], core_in.at[k], core_sems, (k,), twin
        )

    def return_pair(k):
        if k < 0:
            return
        returns[k, "core"].wait_recv()
        per = rows // step

        def target(i):
            at = pl.ds(pl.multiple_of(core * rows + i % per * step, step), step)
            return (k, i // per // 2, i // per % 2, at)

        def source(i):
            at = pl.ds(pl.multiple_of(i % per * step, step), step)
            return core_in, (k, i // per // 2, i // per % 2, at)

        add_rows(4 * per, target, source)
        returns[k, "a"] = send(
            parts.at[k, 1 - y, :, half_rows[0]], pair_in.at[k, 0], pair_sems, (k, 0), across_y
        )
        returns[k, "b"] = send(
            parts.at[k, :, 1 - x, half_rows[1]], pair_in.at[k, 1], pair_sems, (k, 1), across_x
        )

    def return_last(k):
        if k < 0:
            return
        per = half // step
        for t in range(2):
            returns[k, "ab"[t]].wait_recv()

            def target(i, t=t):
                at = pl.ds(pl.multiple_of(core * rows + t * half + i % per * step, step), step)
                return (k, y, i // per, at) if t == 0 else (k, i // per, x, at)

            def source(i, t=t):
                at = pl.ds(pl.multiple_of(i % per * step, step), step)
                return pair_in, (k, t, i // per, at)

            add_rows(2 * per, target, source)
        returns[k, "c"] = send(
            parts.at[k, y, 1 - x, half_rows[0]], last_in.at[k, 0], last_sems, (k, 0), across_x
        )
        returns[k, "d"] = send(
            parts.at[k, 1 - y, x, half_rows[1]], last_in.at[k, 1], last_sems, (k, 1), across_y
        )

    def return_plane(k):
        if k < 0:
            return
        per = half // step
        for t in range(2):
            returns[k, "cd"[t]].wait_recv()

            def target(i, t=t):
                at = pl.ds(pl.multiple_of(core * rows + t * half + i * step, step), step)
                return (k, y, x, at)

            def source(i, t=t):
                at = pl.ds(pl.multiple_of(i * step, step), step)
                return last_in, (k, t, at)

            add_rows(per, target, source)
        if k > 0:
            returns[k, "z"] = send(
                parts.at[k, y, x, own_rows],
                plane_in.at[k],
                back_sems,
                (k,),
                {"grp": lax.rem(z + k, planes)},
            )

    def scale_rows(ref, scales):
        groups = scales.shape[0]
        size = ref.shape[0] // groups

        def one(g, carry):
            at = pl.ds(pl.multiple_of(g * size, size), size)
            ref[at] = (ref[at].astype(f32) * jnp.where(is_hot, 1.0, scales[pl.ds(g, 1), :])).astype(bf16)
            return carry

        lax.fori_loop(0, groups, one, 0)

    first_spread(0)
    loads[0].wait()
    scale_rows(gate_up.at[0], gate_up_scale_ref.at[0])
    second_spread(0)
    first_spread(1)
    loads[1].wait()
    scale_rows(gate_up.at[1], gate_up_scale_ref.at[1])
    loads[2].wait()
    scale_rows(down, down_scale_ref)
    to_twin(0)
    second_spread(1)

    for k in range(planes):
        for later in range(k + 3, planes if k == 0 else k + 3):
            to_plane(later)
        first_spread(k + 2)
        if k > 2:
            return_pair(k - 1)
        twins[k].wait_recv()
        gate_up_phase(k, 0)
        down_phase(k, 0)
        to_twin(k + 1)
        second_spread(k + 2)
        if k == planes - 1:
            return_pair(0)
            return_last(1)
        gate_up_phase(k, 1)
        down_phase(k, 1)
        return_core(k)
        if k == 2:
            return_pair(1)
    return_pair(planes - 1)
    for k in range(2, planes):
        return_last(k)
        return_plane(k - 1)
    return_last(0)
    return_plane(planes - 1)
    return_plane(0)
    for k in range(1, planes):
        returns[k, "z"].wait_recv()

    def finish(i, carry):
        at = pl.ds(pl.multiple_of(i * step, step), step)
        mine = pl.ds(pl.multiple_of(core * rows + i * step, step), step)
        total = parts[0, y, x, mine].astype(f32)
        for k in range(1, planes):
            total = total + plane_in[k, at].astype(f32)
        out_ref[at] = total.astype(bf16)
        return carry

    lax.fori_loop(0, rows // step, finish, 0)
    for copy in pending:
        copy.wait_send()


def dense_shards(
    tokens, expert_ids, combine, hot_flags, gate_up_weight, gate_up_scale, down_weight, down_scale
):
    planes = lax.axis_size("grp")
    lane_count = lax.axis_size("ex")
    expert_count = planes // 2 * lane_count
    rows, width = tokens.shape
    units = down_weight.shape[2]
    named = expert_ids[:, :, None] == jnp.arange(expert_count, dtype=jnp.int32)
    coefficient = jnp.sum(jnp.where(named, combine[:, :, None], 0.0), axis=1)
    pieces, rest = [], coefficient
    for _ in range(3):
        piece = lax.reduce_precision(rest, 8, 7)
        pieces.append(piece.astype(jnp.bfloat16))
        rest = rest - piece
    extra = -(-3 * expert_count // 128) * 128
    blank = jnp.zeros((rows, extra - 3 * expert_count), jnp.bfloat16)
    own_rows = jnp.concatenate([tokens] + pieces + [blank], axis=1)
    bf16 = jnp.bfloat16
    dma = pltpu.SemaphoreType.DMA
    return pl.pallas_call(
        functools.partial(fused_kernel, planes, expert_count),
        out_shape=jax.ShapeDtypeStruct((rows, width), bf16),
        in_specs=[
            pl.BlockSpec(memory_space=pltpu.SMEM),
            pl.BlockSpec(memory_space=pl.ANY),
            pl.BlockSpec(memory_space=pl.ANY),
            pl.BlockSpec(memory_space=pltpu.VMEM),
            pl.BlockSpec(memory_space=pl.ANY),
            pl.BlockSpec(memory_space=pltpu.VMEM),
        ],
        out_specs=pl.BlockSpec(memory_space=pltpu.VMEM),
        scratch_shapes=[
            pltpu.VMEM((planes, 2, 2, 2 * rows, width + extra), bf16),
            pltpu.VMEM((planes, 2, 2, 2 * rows, width), bf16),
            pltpu.VMEM((planes, 2, 2, rows, width), bf16),
            pltpu.VMEM((planes, 2, 2, rows // 2, width), bf16),
            pltpu.VMEM((planes, 2, rows // 2, width), bf16),
            pltpu.VMEM((planes, rows, width), bf16),
            pltpu.VMEM((2, width, units), bf16),
            pltpu.VMEM((units, width), bf16),
            pltpu.VMEM((4 * rows, units), bf16),
            dma((4,)),
            dma((2, planes)),
            dma((2, planes, 2, 3)),
            dma((2, planes)),
            dma((2, planes)),
            dma((2, planes, 2)),
            dma((2, planes, 2)),
            dma((2, planes)),
        ],
        compiler_params=pltpu.CompilerParams(
            collective_id=0, has_side_effects=True, vmem_limit_bytes=67043328
        ),
    )(
        hot_flags,
        own_rows,
        gate_up_weight[0, 0],
        gate_up_scale[0, 0],
        down_weight[0, 0],
        down_scale[0, 0],
    )


def shards(tokens, expert_ids, *rest):
    group_count = lax.axis_size("grp")
    lane_count = lax.axis_size("ex")
    token_count = tokens.shape[0]
    expert_count = group_count // 2 * lane_count
    route_count = token_count * expert_ids.shape[1]
    capacity = max(2, (5 * route_count + 4 * expert_count - 1) // (4 * expert_count))
    chip_rows = group_count * lane_count // 2 * token_count
    if lane_count == 2 * 2 * 2 and 2 * expert_count * capacity >= chip_rows:
        return dense_shards(tokens, expert_ids, *rest)
    return routed_shards(tokens, expert_ids, *rest)


def solution(mesh):
    return jax.shard_map(
        shards,
        mesh=mesh,
        in_specs=(
            P(("grp", "ex"), None),
            P(("grp", "ex"), None),
            P(("grp", "ex"), None),
            P(),
            P("grp", "ex", None, None, None),
            P("grp", "ex", None, None, None),
            P("grp", "ex", None, None),
            P("grp", "ex", None, None),
        ),
        out_specs=P(("grp", "ex"), None),
        check_vma=False,
    )
```
